32 devices in a mesh: leaf: 4 (over z), front: 8 (over y, x, core).
Axes of the slice: x: 2, y: 2, z: 4, core: 2. Of those that a mesh axis runs over, the one named last changes fastest.
Arguments:
- rhs_leaf: float32 [4, 2048, 64], P('leaf', 'front'), may hold values from -2.4 to 2.4
- diag_inv: bfloat16 [4, 8, 256, 256], P('leaf', 'front'), as said below
- sub_block: bfloat16 [4, 8, 256, 256], P('leaf', 'front'), as said below
- coupling: bfloat16 [4, 256, 2048], P('leaf', None, 'front'), may hold values from -0.25 to 0.25
- update_rows: int32 [4, 256], P('leaf'), may hold values from 0 to 1023, as said below
- rhs_sep: float32 [1024, 64], P('leaf'), may hold values from -6 to 6
- sep_inv: bfloat16 [1024, 1024], P('front', 'leaf'), as said below
Outputs:
- leaf_solution: float32 [4, 2048, 64], P('leaf', 'front')
- separator_solution: float32 [1024, 64], P('leaf')
The draws below stay inside these ranges and needn't reach their ends.
Inputs may be any that keep to these rules, and one draw needn't show every extreme that they name: `update_rows`: within a group the 256 indices are distinct and increasing, and include the first and the last separator row. `diag_inv`: each 256 x 256 block is lower triangular. `sub_block`: each 256 x 256 block is lower triangular. `sep_inv`: lower triangular.
All inputs are finite; a program needn't handle non-finite values.
Results may differ from the reference program's by a relative error of at most 0.0003.
Values may be sent and summed in bfloat16 or wider, within the bound.
A program may use at most 64 MiB of HBM per device.

```python
import math
import jax
import jax.numpy as jnp
from jax import lax

W = 256
R = 64
U = 256
S = 1024
SUBTREE_GROUPS = 4
CHAIN_SUPERNODES = 8
ROWS = 2048


def factor_parts(key):
    folded = jax.random.fold_in(key, 11)
    parallel_lanes = jax.random.split(folded, 8)
    slow_share = 0.5
    is_slow = jax.random.bernoulli(parallel_lanes[0], slow_share, (SUBTREE_GROUPS, 1, W))
    survive = jax.random.uniform(parallel_lanes[1], (SUBTREE_GROUPS, 1, 1), minval=0.15, maxval=0.3)
    per_step = jnp.exp(jnp.log(survive / 0.36) / CHAIN_SUPERNODES)
    jitter = jax.random.uniform(parallel_lanes[2], (SUBTREE_GROUPS, CHAIN_SUPERNODES, 1), minval=0.5, maxval=1.5)
    slow_rate = per_step ** jitter
    spread_begin = jax.random.randint(parallel_lanes[3], (SUBTREE_GROUPS, 2), 0, CHAIN_SUPERNODES)
    current_place = jnp.arange(CHAIN_SUPERNODES)
    spreading_active = jnp.any(current_place[None, :, None] == spread_begin[:, None, :], axis=2)[:, :, None]
    slow_rate = jnp.where(spreading_active, 0.6 * slow_rate, slow_rate)
    fast_rate = jax.random.uniform(parallel_lanes[4], (SUBTREE_GROUPS, CHAIN_SUPERNODES, W), minval=0.2, maxval=0.6)
    decay_rate = jnp.where(is_slow, slow_rate, fast_rate)
    pivots = jnp.exp(jax.random.uniform(parallel_lanes[5], (SUBTREE_GROUPS, CHAIN_SUPERNODES, W), minval=math.log(0.7), maxval=math.log(1.4)))
    identity_w = jnp.eye(W, dtype=jnp.float32)
    lower_first = jnp.tril(jax.random.normal(parallel_lanes[6], (SUBTREE_GROUPS, CHAIN_SUPERNODES, W, W)) * (0.3 / math.sqrt(W)), -1)
    lower_second = jnp.tril(jax.random.normal(parallel_lanes[7], (SUBTREE_GROUPS, CHAIN_SUPERNODES, W, W)) * (0.3 / math.sqrt(W)), -1)
    inverse_part = lower_first + pivots[..., None] * identity_w
    couple_part = lower_second + (-decay_rate / pivots)[..., None] * identity_w
    return (inverse_part, couple_part)


def draw_diag_inv(key, part):
    inverse_part, couple_part = factor_parts(key)
    return inverse_part.astype(jnp.bfloat16)


def draw_sub_block(key, part):
    inverse_part, couple_part = factor_parts(key)
    return couple_part.astype(jnp.bfloat16)


def draw_update_rows(key, part):
    parallel_lanes = jax.random.split(jax.random.fold_in(key, 5), SUBTREE_GROUPS)
    middle = jax.vmap(lambda stream: jax.random.permutation(stream, S - 2))(parallel_lanes)[:, :U - 2] + 1
    leading_row = jnp.zeros((SUBTREE_GROUPS, 1), jnp.int32)
    last_row = jnp.full((SUBTREE_GROUPS, 1), S - 1, jnp.int32)
    chosen = jnp.concatenate([leading_row, middle.astype(jnp.int32), last_row], axis=1)
    return jnp.sort(chosen, axis=1).astype(jnp.int32)


def draw_sep_inv(key, part):
    parallel_lanes = jax.random.split(jax.random.fold_in(key, 23), 2)
    random_part = jax.random.normal(parallel_lanes[0], (S, S))
    lower_part = jnp.tril(random_part * (0.5 / math.sqrt(S)), -1)
    diagonal = jnp.exp(jax.random.uniform(parallel_lanes[1], (S,), minval=math.log(0.5), maxval=math.log(2.0)))
    return (lower_part + diagonal[:, None] * jnp.eye(S, dtype=jnp.float32)).astype(jnp.bfloat16)


def level_of(key, extent, shards, least, largest):
    gain = 1.0
    for axis_at, blocks in shards:
        heights = jax.random.uniform(jax.random.fold_in(jax.random.fold_in(key, 6), axis_at), (blocks,), jnp.float32, least / len(shards), largest / len(shards))
        gain = gain * jnp.repeat(jnp.exp(heights), extent[axis_at] // blocks).reshape((-1,) + (1,) * (len(extent) - 1 - axis_at))
    return gain


def normal_values(key, dims, scale, most, pieces=(), held_as=jnp.bfloat16):
    level = level_of(key, dims, pieces, -0.22, 0.18) if pieces else 1.0
    array = jax.random.normal(key, dims, jnp.float32) * scale * level
    return jnp.minimum(jnp.maximum(array, -most), most).astype(held_as)


def setup_inputs(seed: int = 0) -> dict:
    arg_keys = jax.random.split(jax.random.key(seed), 8)
    rhs_leaf = normal_values(arg_keys[0], (SUBTREE_GROUPS, ROWS, R), 0.3, 2.4, ((0, 4), (1, 8)), jnp.float32)
    diag_inv = draw_diag_inv(jax.random.fold_in(arg_keys[7], 71), 0)
    sub_block = draw_sub_block(jax.random.fold_in(arg_keys[7], 71), 0)
    coupling = normal_values(arg_keys[3], (SUBTREE_GROUPS, U, ROWS), (ROWS // 4) ** -0.5, 0.25, ((0, 4), (2, 8)))
    update_rows = draw_update_rows(jax.random.fold_in(arg_keys[7], 71), 0)
    rhs_sep = normal_values(arg_keys[5], (S, R), 1.0, 6.0, ((0, 4),), jnp.float32)
    sep_inv = draw_sep_inv(jax.random.fold_in(arg_keys[7], 71), 0)
    return {"rhs_leaf": rhs_leaf, "diag_inv": diag_inv, "sub_block": sub_block, "coupling": coupling, "update_rows": update_rows, "rhs_sep": rhs_sep, "sep_inv": sep_inv}


PRECISE = lax.Precision.HIGHEST


def product(left, right):
    return jnp.matmul(left, right, precision=PRECISE)


def reference(rhs_leaf, diag_inv, sub_block, coupling, update_rows, rhs_sep, sep_inv):
    blocks = rhs_leaf.reshape(SUBTREE_GROUPS, CHAIN_SUPERNODES, W, R)

    def forward_group(inputs):
        inverses, couples, rights = inputs

        def advance(previous, item):
            inverse, couple, right = item
            value = product(inverse.astype(jnp.float32), right - product(couple.astype(jnp.float32), previous))
            return value, value

        _, values = lax.scan(advance, jnp.zeros((W, R), jnp.float32), (inverses, couples, rights))
        return values.reshape(ROWS, R)

    forward_y = lax.map(forward_group, (diag_inv, sub_block, blocks))

    def group_update(inputs):
        block_rows, values = inputs
        return product(block_rows.astype(jnp.float32), values)

    updates = lax.map(group_update, (coupling, forward_y))
    update_total = jnp.zeros((S, R), jnp.float32).at[update_rows.reshape(-1)].add(updates.reshape(SUBTREE_GROUPS * U, R))
    inverse_sep = sep_inv.astype(jnp.float32)
    sep_forward = product(inverse_sep, rhs_sep - update_total)
    separator_solution = product(inverse_sep.T, sep_forward)

    def backward_group(inputs):
        inverses, couples, values, block_rows, indices = inputs
        selected_entries = separator_solution[indices]
        adjusted = values - product(block_rows.astype(jnp.float32).T, selected_entries)
        following = jnp.concatenate([couples[1:], jnp.zeros((1, W, W), couples.dtype)], axis=0)

        def retreat(later, item):
            inverse, couple, right = item
            value = product(inverse.astype(jnp.float32).T, right - product(couple.astype(jnp.float32).T, later))
            return value, value

        _, solved = lax.scan(retreat, jnp.zeros((W, R), jnp.float32), (inverses, following, adjusted.reshape(CHAIN_SUPERNODES, W, R)), reverse=True)
        return solved.reshape(ROWS, R)

    leaf_solution = lax.map(backward_group, (diag_inv, sub_block, forward_y, coupling, update_rows))
    return leaf_solution, separator_solution
```

```python
import functools

import jax
import jax.numpy as jnp
from jax import lax
from jax.experimental import pallas as pl
from jax.experimental.pallas import tpu as pltpu
from jax.sharding import PartitionSpec as P

MESH = pl.DeviceIdType.MESH
F32 = jnp.float32
BF16 = jnp.bfloat16


def halves(x):
    head = x.astype(BF16)
    rest = (x - head.astype(F32)).astype(BF16)
    return jnp.concatenate([head, rest], axis=0)


def joined(both):
    rows = both.shape[0] // 2
    return both[:rows] + both[rows:]


def times(x, w):
    return joined(jnp.dot(halves(x), w, preferred_element_type=F32))


def times_t(x, w):
    dims = (((1,), (1,)), ((), ()))
    return joined(lax.dot_general(halves(x), w, dims, preferred_element_type=F32))


def kernel(
    groups, chips, skips,
    r_ref, d_ref, b_ref, c_ref, idx_ref, rs_ref, sp_ref,
    out_ref, sol_ref,
    fac, rt, rbuf, ybuf, yin, uin, uout, ubuf, rst, rsbuf, idxbuf, sepbuf, sel, ssep, solt,
    zbuf, solbuf, vin, vout, xs, obuf,
    loc_s, swap_s, swap_r, y_s, y_r, u_s, u_r, v_s, v_r,
    ux_s, ux_r, rs_s, rs_r, id_s, id_r, sep_s, sep_r, fwd_s, fwd_r,
    z_s, z_r, so_s, so_r, x_s, x_r, sx_s, sx_r,
):
    plane = lax.axis_index("leaf")
    front = lax.axis_index("front")
    chip = front // 2
    core = front % 2
    other = 1 - core
    last = chips - 1
    is_last = chip == last
    sibling = (plane, chip * 2 + other)
    half = rbuf.shape[1]
    wide = solt.shape[1] // groups
    deep = sepbuf.shape[3]

    def remote(src, dst, send, recv, to):
        return pltpu.make_async_remote_copy(
            src_ref=src, dst_ref=dst, send_sem=send, recv_sem=recv, device_id=to, device_id_type=MESH
        )

    barrier = pltpu.get_barrier_semaphore()

    def greet(to):
        pl.semaphore_signal(barrier, inc=1, device_id=to, device_id_type=MESH)

    greet(sibling)

    @pl.when(is_last)
    def _():
        for g in range(groups):
            for c in range(chips):
                if c < last:
                    greet((g, c * 2 + core))
                else:
                    @pl.when(plane != g)
                    def _(g=g, c=c):
                        greet((g, c * 2 + core))

    @pl.when(jnp.logical_not(is_last))
    def _():
        for g in range(groups):
            greet((g, last * 2 + core))

        @pl.when(chip > 0)
        def _():
            greet((plane, front - 2))

        @pl.when(chip + 1 < last)
        def _():
            greet((plane, front + 2))

    near = (chip > 0).astype(jnp.int32) + (chip + 1 < last).astype(jnp.int32)
    pl.semaphore_wait(barrier, jnp.where(is_last, groups * chips, groups + 1 + near))

    swaps = []
    locals_ = []
    for i, ref in enumerate((b_ref, d_ref, c_ref)):
        copy = remote(ref, fac.at[i, core], swap_s.at[i], swap_r.at[i], sibling)
        copy.start()
        swaps.append(copy)
        copy = pltpu.make_async_copy(ref, fac.at[i, core], loc_s.at[i])
        copy.start()
        locals_.append(copy)
    flipped = r_ref[...].T
    rt[0] = flipped[:half]
    rt[1] = flipped[half:]
    rbuf[core] = rt[core]
    copy = remote(rt.at[other], rbuf.at[core], swap_s.at[3], swap_r.at[3], sibling)
    copy.start()
    swaps.append(copy)

    def sep_copies(g):
        return remote(
            sp_ref, sepbuf.at[plane, core, chip], sep_s.at[g], sep_r.at[plane], (g, last * 2 + core)
        )

    useful = chip >= (plane * wide) // (2 * deep)
    for g in range(groups):
        mine = jnp.logical_and(is_last, plane == g)

        @pl.when(jnp.logical_and(useful, jnp.logical_not(mine)))
        def _(g=g):
            sep_copies(g).start()

        @pl.when(mine)
        def _(g=g):
            pltpu.make_async_copy(sp_ref, sepbuf.at[g, core, last], sep_r.at[g]).start()

    def peers(action):
        for g in range(groups):
            @pl.when(plane != g)
            def _(g=g):
                action(g, (g, last * 2 + core))

    @pl.when(is_last)
    def _():
        upright = rs_ref[...].T
        rst[0] = upright[:half]
        rst[1] = upright[half:]
        rsbuf[plane] = rst[core]
        idxbuf[plane] = idx_ref[...]

        def give(g, to):
            remote(rst.at[core], rsbuf.at[plane], rs_s.at[g], rs_r.at[plane], to).start()
            remote(idx_ref, idxbuf.at[plane], id_s.at[g], id_r.at[plane], to).start()

        peers(give)

    for copy in locals_:
        copy.wait()
    for copy in swaps:
        copy.wait_recv()

    @pl.when(is_last)
    def _():
        def take(g, to):
            remote(idx_ref, idxbuf.at[g], id_s.at[g], id_r.at[g], to).wait_recv()
            remote(rst.at[core], rsbuf.at[g], rs_s.at[g], rs_r.at[g], to).wait_recv()

        peers(take)
        for g in range(groups):
            rows = lax.broadcasted_iota(jnp.int32, sel.shape[1:], 0)
            sel[g] = (rows == idxbuf[g]).astype(F32).astype(BF16)
        for g in range(groups):
            part = sepbuf.at[g, core, pl.ds(skips[g], chips - skips[g])]
            pltpu.make_async_copy(part, part, sep_r.at[g]).wait()
            remote(part, part, fwd_s.at[g], fwd_r.at[g], sibling).start()

    @pl.when(chip == 0)
    def _():
        yin[...] = jnp.zeros_like(yin)
        uin[...] = jnp.zeros_like(uin)

    onward = (plane, jnp.minimum(front + 2, last * 2 + core))
    behind = (plane, jnp.maximum(front - 2, core))
    y_copy = remote(ybuf.at[1], yin, y_s, y_r, onward)
    u_copy = remote(uout, uin, u_s, u_r, onward)

    @pl.when(chip > 0)
    def _():
        y_copy.wait_recv()

    first = times_t(rbuf[0] - times_t(yin[...], fac[0, 0]), fac[1, 0])
    second = times_t(rbuf[1] - times_t(first, fac[0, 1]), fac[1, 1])
    ybuf[0] = first
    ybuf[1] = second

    @pl.when(jnp.logical_not(is_last))
    def _():
        y_copy.start()

    update = times_t(first, fac[2, 0]) + times_t(second, fac[2, 1])

    @pl.when(chip > 0)
    def _():
        u_copy.wait_recv()

    uout[...] = update + uin[...]

    @pl.when(jnp.logical_not(is_last))
    def _():
        u_copy.start()

    z_copies = [
        remote(zbuf, zbuf, z_s.at[c], z_r, (plane, c * 2 + core)) for c in range(last)
    ]
    so_copies = [
        remote(solbuf.at[core], solbuf.at[core], so_s.at[c], so_r, (plane, c * 2 + core))
        for c in range(last)
    ]

    @pl.when(is_last)
    def _():
        ubuf[plane] = uout[...]
        peers(lambda g, to: remote(uout, ubuf.at[plane], ux_s.at[g], ux_r.at[plane], to).start())
        for g in range(groups):
            part = sepbuf.at[g, other, pl.ds(skips[g], chips - skips[g])]
            remote(part, part, fwd_s.at[g], fwd_r.at[g], sibling).wait_recv()
        peers(lambda g, to: remote(uout, ubuf.at[g], ux_s.at[g], ux_r.at[g], to).wait_recv())
        total = times_t(ubuf[0], sel[0])
        for g in range(1, groups):
            total = total + times_t(ubuf[g], sel[g])
        ssep[...] = jnp.zeros_like(ssep)
        for g in range(groups):
            part = halves(rsbuf[g] - total[:, g * wide : (g + 1) * wide])
            for k in range(2):
                block = sepbuf[g, k, skips[g] :].reshape((chips - skips[g]) * deep, wide)
                ssep[k, :, skips[g] * deep :] += joined(
                    lax.dot_general(part, block, (((1,), (1,)), ((), ())), preferred_element_type=F32)
                )
        for g in range(groups):
            part = 0
            for k in range(2):
                block = sepbuf[g, k, skips[g] :].reshape((chips - skips[g]) * deep, wide)
                part = part + times(ssep[k, :, skips[g] * deep :], block)
            solt[:, g * wide : (g + 1) * wide] = part

            @pl.when(plane == g)
            def _(part=part):
                solbuf[core] = part

        zbuf[...] = times(solt[...], sel[plane])
        for copy in reversed(z_copies):
            copy.start()
        for copy in so_copies:
            copy.start()

    @pl.when(jnp.logical_not(is_last))
    def _():
        z_copies[0].wait_recv()

    picked = halves(zbuf[...])
    a_first = ybuf[0] - joined(jnp.dot(picked, fac[2, 0], preferred_element_type=F32))
    a_second = ybuf[1] - joined(jnp.dot(picked, fac[2, 1], preferred_element_type=F32))
    v_copy = remote(vout, vin, v_s, v_r, behind)

    @pl.when(is_last)
    def _():
        vin[...] = jnp.zeros_like(vin)

    @pl.when(jnp.logical_not(is_last))
    def _():
        v_copy.wait_recv()

    x_second = times(a_second - vin[...], fac[1, 1])
    x_first = times(a_first - times(x_second, fac[0, 1]), fac[1, 0])

    @pl.when(chip > 0)
    def _():
        vout[...] = times(x_first, fac[0, 0])
        v_copy.start()

    xs[0] = x_first
    xs[1] = x_second
    obuf[core] = xs[core]
    x_copy = remote(xs.at[other], obuf.at[core], x_s, x_r, sibling)
    x_copy.start()

    @pl.when(jnp.logical_not(is_last))
    def _():
        so_copies[0].wait_recv()

    sx_copy = remote(solbuf.at[core], solbuf.at[core], sx_s, sx_r, sibling)
    sx_copy.start()
    x_copy.wait_recv()
    for k in range(2):
        out_ref[k * half : (k + 1) * half] = obuf[k]
    sx_copy.wait_recv()
    for k in range(2):
        sol_ref[k * half : (k + 1) * half] = solbuf[k]

    for copy in swaps:
        copy.wait_send()
    for g in range(groups):
        mine = jnp.logical_and(is_last, plane == g)

        @pl.when(jnp.logical_and(useful, jnp.logical_not(mine)))
        def _(g=g):
            sep_copies(g).wait_send()

    @pl.when(jnp.logical_not(is_last))
    def _():
        y_copy.wait_send()
        u_copy.wait_send()

    @pl.when(chip > 0)
    def _():
        v_copy.wait_send()

    @pl.when(is_last)
    def _():
        def sent(g, to):
            remote(rst.at[core], rsbuf.at[plane], rs_s.at[g], rs_r.at[plane], to).wait_send()
            remote(idx_ref, idxbuf.at[plane], id_s.at[g], id_r.at[plane], to).wait_send()
            remote(uout, ubuf.at[plane], ux_s.at[g], ux_r.at[plane], to).wait_send()

        peers(sent)
        for g in range(groups):
            part = sepbuf.at[g, core, pl.ds(skips[g], chips - skips[g])]
            remote(part, part, fwd_s.at[g], fwd_r.at[g], sibling).wait_send()
        for copy in z_copies:
            copy.wait_send()
        for copy in so_copies:
            copy.wait_send()

    x_copy.wait_send()
    sx_copy.wait_send()


def solution(mesh):
    groups, fronts = mesh.shape["leaf"], mesh.shape["front"]
    chips = fronts // 2

    def shards(rhs_leaf, diag_inv, sub_block, coupling, update_rows, rhs_sep, sep_inv):
        width, columns = rhs_leaf.shape[1:]
        picks = coupling.shape[1]
        wide = rhs_sep.shape[0]
        deep = sep_inv.shape[0]
        rows = wide * groups
        half = columns // 2
        skips = tuple(g * wide // (2 * deep) for g in range(groups))
        vmem = pl.BlockSpec(memory_space=pltpu.VMEM)
        anywhere = pl.BlockSpec(memory_space=pl.ANY)
        dma = pltpu.SemaphoreType.DMA
        out, sol = pl.pallas_call(
            functools.partial(kernel, groups, chips, skips),
            out_shape=(
                jax.ShapeDtypeStruct((columns, width), F32),
                jax.ShapeDtypeStruct((columns, wide), F32),
            ),
            in_specs=[vmem, anywhere, anywhere, anywhere, vmem, vmem, anywhere],
            out_specs=(vmem, vmem),
            scratch_shapes=[
                pltpu.VMEM((3, 2, width, width), BF16),
                pltpu.VMEM((2, half, width), F32),
                pltpu.VMEM((2, half, width), F32),
                pltpu.VMEM((2, half, width), F32),
                pltpu.VMEM((half, width), F32),
                pltpu.VMEM((half, picks), F32),
                pltpu.VMEM((half, picks), F32),
                pltpu.VMEM((groups, half, picks), F32),
                pltpu.VMEM((2, half, wide), F32),
                pltpu.VMEM((groups, half, wide), F32),
                pltpu.VMEM((groups, 1, picks), jnp.int32),
                pltpu.VMEM((groups, 2, chips, deep, wide), BF16),
                pltpu.VMEM((groups, rows, picks), BF16),
                pltpu.VMEM((2, half, chips * deep), F32),
                pltpu.VMEM((half, rows), F32),
                pltpu.VMEM((half, picks), F32),
                pltpu.VMEM((2, half, wide), F32),
                pltpu.VMEM((half, width), F32),
                pltpu.VMEM((half, width), F32),
                pltpu.VMEM((2, half, width), F32),
                pltpu.VMEM((2, half, width), F32),
                dma((3,)), dma((4,)), dma((4,)), dma, dma, dma, dma, dma, dma,
                dma((groups,)), dma((groups,)), dma((groups,)), dma((groups,)),
                dma((groups,)), dma((groups,)), dma((groups,)), dma((groups,)),
                dma((groups,)), dma((groups,)),
                dma((chips,)), dma, dma((chips,)), dma, dma, dma, dma, dma,
            ],
            compiler_params=pltpu.CompilerParams(
                collective_id=0, has_side_effects=True, vmem_limit_bytes=40 * 1024 * 1024
            ),
        )(
            rhs_leaf[0], diag_inv[0, 0], sub_block[0, 0], coupling[0],
            update_rows, rhs_sep, sep_inv,
        )
        return out.T[None], sol.T

    return jax.shard_map(
        shards,
        mesh=mesh,
        in_specs=(
            P("leaf", "front", None),
            P("leaf", "front", None, None),
            P("leaf", "front", None, None),
            P("leaf", None, "front"),
            P("leaf", None),
            P("leaf", None),
            P("front", "leaf"),
        ),
        out_specs=(P("leaf", "front", None), P("leaf", None)),
        check_vma=False,
    )
```

```python
import functools

import jax
import jax.numpy as jnp
from jax import lax
from jax.experimental import pallas as pl
from jax.experimental.pallas import tpu as pltpu
from jax.sharding import PartitionSpec as P

MESH = pl.DeviceIdType.MESH
F32 = jnp.float32
BF16 = jnp.bfloat16


def halves(x):
    head = x.astype(BF16)
    rest = (x - head.astype(F32)).astype(BF16)
    return jnp.concatenate([head, rest], axis=0)


def joined(both):
    rows = both.shape[0] // 2
    return both[:rows] + both[rows:]


def times(x, w):
    return joined(jnp.dot(halves(x), w, preferred_element_type=F32))


def times_t(x, w):
    dims = (((1,), (1,)), ((), ()))
    return joined(lax.dot_general(halves(x), w, dims, preferred_element_type=F32))


def dot(a, b):
    return jnp.dot(a, b, preferred_element_type=F32)


def dot_t(a, b):
    return lax.dot_general(a, b, (((1,), (1,)), ((), ())), preferred_element_type=F32)


def split(x):
    head = x.astype(BF16)
    return head, (x - head.astype(F32)).astype(BF16)


def through(x, w, multiply):
    both = halves(x)
    return joined(multiply(both, w[0])) + multiply(both[: x.shape[0]], w[1])


def kernel(
    groups, chips, skips,
    r_ref, d_ref, b_ref, c_ref, idx_ref, rs_ref, sp_ref,
    out_ref, sol_ref,
    fac, gmap, hmap, rbuf, ybuf, yin, uin, uout, ubuf, rsbuf, idxbuf, sepbuf, sel, ssep, solt,
    zbuf, solbuf, vin, vout, xs, obuf,
    loc_s, swap_s, swap_r, y_s, y_r, u_s, u_r, v_s, v_r,
    ux_s, ux_r, rs_s, rs_r, id_s, id_r, sep_s, sep_r, fwd_s, fwd_r,
    z_s, z_r, so_s, so_r, x_s, x_r, sx_s, sx_r,
):
    plane = lax.axis_index("leaf")
    front = lax.axis_index("front")
    chip = front // 2
    core = front % 2
    other = 1 - core
    last = chips - 1
    is_last = chip == last
    sibling = (plane, chip * 2 + other)
    half = rbuf.shape[1]
    wide = solt.shape[1] // groups
    deep = sepbuf.shape[3]

    def remote(src, dst, send, recv, to):
        return pltpu.make_async_remote_copy(
            src_ref=src, dst_ref=dst, send_sem=send, recv_sem=recv, device_id=to, device_id_type=MESH
        )

    barrier = pltpu.get_barrier_semaphore()

    def greet(to):
        pl.semaphore_signal(barrier, inc=1, device_id=to, device_id_type=MESH)

    greet(sibling)

    @pl.when(is_last)
    def _():
        for g in range(groups):
            for c in range(chips):
                if c < last:
                    greet((g, c * 2 + core))
                else:
                    @pl.when(plane != g)
                    def _(g=g, c=c):
                        greet((g, c * 2 + core))

    @pl.when(jnp.logical_not(is_last))
    def _():
        for g in range(groups):
            greet((g, last * 2 + core))

        @pl.when(chip > 0)
        def _():
            greet((plane, front - 2))

        @pl.when(chip + 1 < last)
        def _():
            greet((plane, front + 2))

    near = (chip > 0).astype(jnp.int32) + (chip + 1 < last).astype(jnp.int32)
    pl.semaphore_wait(barrier, jnp.where(is_last, groups * chips, groups + 1 + near))

    swaps = []
    locals_ = []
    for i, ref in enumerate((b_ref, d_ref, c_ref)):
        copy = remote(ref, fac.at[i, core], swap_s.at[i], swap_r.at[i], sibling)
        copy.start()
        swaps.append(copy)
        copy = pltpu.make_async_copy(ref, fac.at[i, core], loc_s.at[i])
        copy.start()
        locals_.append(copy)
    mine_rows = pl.ds(pl.multiple_of(core * half, half), half)
    other_rows = pl.ds(pl.multiple_of(other * half, half), half)
    rbuf[core] = r_ref[mine_rows]
    copy = remote(r_ref.at[other_rows], rbuf.at[core], swap_s.at[3], swap_r.at[3], sibling)
    copy.start()
    swaps.append(copy)

    def sep_copies(g):
        return remote(
            sp_ref, sepbuf.at[plane, core, chip], sep_s.at[g], sep_r.at[plane], (g, last * 2 + core)
        )

    useful = chip >= (plane * wide) // (2 * deep)
    for g in range(groups):
        mine = jnp.logical_and(is_last, plane == g)

        @pl.when(jnp.logical_and(useful, jnp.logical_not(mine)))
        def _(g=g):
            sep_copies(g).start()

        @pl.when(mine)
        def _(g=g):
            pltpu.make_async_copy(sp_ref, sepbuf.at[g, core, last], sep_r.at[g]).start()

    def peers(action):
        for g in range(groups):
            @pl.when(plane != g)
            def _(g=g):
                action(g, (g, last * 2 + core))

    @pl.when(is_last)
    def _():
        rsbuf[plane] = rs_ref[mine_rows]
        idxbuf[plane] = idx_ref[...]

        def give(g, to):
            remote(rs_ref.at[mine_rows], rsbuf.at[plane], rs_s.at[g], rs_r.at[plane], to).start()
            remote(idx_ref, idxbuf.at[plane], id_s.at[g], id_r.at[plane], to).start()

        peers(give)

    for copy in locals_:
        copy.wait()
    for copy in swaps:
        copy.wait_recv()

    onward = (plane, jnp.minimum(front + 2, last * 2 + core))
    behind = (plane, jnp.maximum(front - 2, core))
    y_copy = remote(ybuf.at[2], yin, y_s, y_r, onward)
    u_copy = remote(uout, uin, u_s, u_r, onward)
    u_copies = []
    for step in range(1, groups):
        g = lax.rem(plane + step, groups)
        u_copies.append(
            remote(uout, ubuf.at[plane], ux_s.at[step - 1], ux_r.at[plane], (g, last * 2 + core))
        )

    own_first = times_t(rbuf[0], fac[1, 0])
    own_second = times_t(rbuf[1] - times_t(own_first, fac[0, 1]), fac[1, 1])

    @pl.when(chip == 0)
    def _():
        yin[...] = jnp.zeros_like(yin)
        uin[...] = jnp.zeros_like(uin)
        ybuf[2] = own_second
        y_copy.start()

    own_update = times_t(own_first, fac[2, 0]) + times_t(own_second, fac[2, 1])
    early = split(dot(fac[1, 0], fac[0, 0]))
    late = split(dot(fac[1, 1], fac[0, 1]))
    whole = split(dot(late[0], early[0]) + (dot(late[1], early[0]) + dot(late[0], early[1])))
    gmap[0], gmap[1] = whole
    seen = split(
        dot(fac[2, 1], whole[0]) - dot(fac[2, 0], early[0])
        + (dot(fac[2, 1], whole[1]) - dot(fac[2, 0], early[1]))
    )
    hmap[0], hmap[1] = seen

    @pl.when(is_last)
    def _():
        def take(g, to):
            remote(idx_ref, idxbuf.at[g], id_s.at[g], id_r.at[g], to).wait_recv()
            remote(rs_ref.at[mine_rows], rsbuf.at[g], rs_s.at[g], rs_r.at[g], to).wait_recv()

        peers(take)
        for g in range(groups):
            rows = lax.broadcasted_iota(jnp.int32, sel.shape[1:], 0)
            sel[g] = (rows == idxbuf[g]).astype(F32).astype(BF16)
        for g in range(groups):
            part = sepbuf.at[g, core, pl.ds(skips[g], chips - skips[g])]
            pltpu.make_async_copy(part, part, sep_r.at[g]).wait()
            remote(part, part, fwd_s.at[g], fwd_r.at[g], sibling).start()

    @pl.when(chip > 0)
    def _():
        y_copy.wait_recv()

    heard = yin[...]
    second = own_second + through(heard, gmap, dot_t)
    ybuf[1] = second

    @pl.when(jnp.logical_and(chip > 0, jnp.logical_not(is_last)))
    def _():
        ybuf[2] = second
        y_copy.start()

    update = own_update + through(heard, hmap, dot_t)

    @pl.when(chip > 0)
    def _():
        u_copy.wait_recv()

    uout[...] = update + uin[...]

    @pl.when(jnp.logical_not(is_last))
    def _():
        u_copy.start()

    @pl.when(is_last)
    def _():
        for step in range(1, groups):
            u_copies[step - 1].start()

    first = own_first - times_t(times_t(heard, fac[0, 0]), fac[1, 0])
    ybuf[0] = first
    turned = times(times(first, fac[1, 0]), fac[0, 0]) - through(second, gmap, dot)

    z_copies = [
        remote(zbuf, zbuf, z_s.at[c], z_r, (plane, c * 2 + core)) for c in range(last)
    ]
    so_copies = [
        remote(solbuf.at[core], solbuf.at[core], so_s.at[c], so_r, (plane, c * 2 + core))
        for c in range(last)
    ]

    @pl.when(is_last)
    def _():
        total = times_t(uout[...], sel[plane])
        for g in range(groups):
            part = sepbuf.at[g, other, pl.ds(skips[g], chips - skips[g])]
            remote(part, part, fwd_s.at[g], fwd_r.at[g], sibling).wait_recv()
        for step in range(1, groups):
            g = lax.rem(plane + step, groups)
            remote(uout, ubuf.at[g], ux_s.at[step - 1], ux_r.at[g], (g, last * 2 + core)).wait_recv()
            total = total + times_t(ubuf[g], sel[g])
        ssep[...] = jnp.zeros_like(ssep)
        for g in range(groups):
            part = halves(rsbuf[g] - total[:, g * wide : (g + 1) * wide])
            for k in range(2):
                block = sepbuf[g, k, skips[g] :].reshape((chips - skips[g]) * deep, wide)
                ssep[k, :, skips[g] * deep :] += joined(
                    lax.dot_general(part, block, (((1,), (1,)), ((), ())), preferred_element_type=F32)
                )
        for g in range(groups):
            part = 0
            for k in range(2):
                block = sepbuf[g, k, skips[g] :].reshape((chips - skips[g]) * deep, wide)
                part = part + times(ssep[k, :, skips[g] * deep :], block)
            solt[:, g * wide : (g + 1) * wide] = part

            @pl.when(plane == g)
            def _(part=part):
                solbuf[core] = part

        zbuf[...] = times(solt[...], sel[plane])
        for copy in reversed(z_copies):
            copy.start()
        for copy in so_copies:
            copy.start()

    @pl.when(jnp.logical_not(is_last))
    def _():
        z_copies[0].wait_recv()

    picked = halves(zbuf[...])
    a_first = ybuf[0] - joined(jnp.dot(picked, fac[2, 0], preferred_element_type=F32))
    a_second = ybuf[1] - joined(jnp.dot(picked, fac[2, 1], preferred_element_type=F32))
    v_copy = remote(vout, vin, v_s, v_r, behind)
    turned = turned + through(zbuf[...], hmap, dot)

    @pl.when(is_last)
    def _():
        vin[...] = jnp.zeros_like(vin)
        vout[...] = turned

    @pl.when(jnp.logical_not(is_last))
    def _():
        v_copy.wait_recv()
        vout[...] = turned + through(vin[...], gmap, dot)

    @pl.when(chip > 0)
    def _():
        v_copy.start()

    x_second = times(a_second - vin[...], fac[1, 1])
    x_first = times(a_first - times(x_second, fac[0, 1]), fac[1, 0])
    xs[0] = x_first
    xs[1] = x_second
    obuf[core] = xs[core]
    x_copy = remote(xs.at[other], obuf.at[core], x_s, x_r, sibling)
    x_copy.start()

    @pl.when(jnp.logical_not(is_last))
    def _():
        so_copies[0].wait_recv()

    sx_copy = remote(solbuf.at[core], solbuf.at[core], sx_s, sx_r, sibling)
    sx_copy.start()
    x_copy.wait_recv()
    for k in range(2):
        out_ref[k * half : (k + 1) * half] = obuf[k]
    sx_copy.wait_recv()
    for k in range(2):
        sol_ref[k * half : (k + 1) * half] = solbuf[k]

    for copy in swaps:
        copy.wait_send()
    for g in range(groups):
        mine = jnp.logical_and(is_last, plane == g)

        @pl.when(jnp.logical_and(useful, jnp.logical_not(mine)))
        def _(g=g):
            sep_copies(g).wait_send()

    @pl.when(jnp.logical_not(is_last))
    def _():
        y_copy.wait_send()
        u_copy.wait_send()

    @pl.when(chip > 0)
    def _():
        v_copy.wait_send()

    @pl.when(is_last)
    def _():
        def sent(g, to):
            remote(rs_ref.at[mine_rows], rsbuf.at[plane], rs_s.at[g], rs_r.at[plane], to).wait_send()
            remote(idx_ref, idxbuf.at[plane], id_s.at[g], id_r.at[plane], to).wait_send()

        peers(sent)
        for copy in u_copies:
            copy.wait_send()
        for g in range(groups):
            part = sepbuf.at[g, core, pl.ds(skips[g], chips - skips[g])]
            remote(part, part, fwd_s.at[g], fwd_r.at[g], sibling).wait_send()
        for copy in z_copies:
            copy.wait_send()
        for copy in so_copies:
            copy.wait_send()

    x_copy.wait_send()
    sx_copy.wait_send()


def solution(mesh):
    groups, fronts = mesh.shape["leaf"], mesh.shape["front"]
    chips = fronts // 2

    def shards(rhs_leaf, diag_inv, sub_block, coupling, update_rows, rhs_sep, sep_inv):
        width, columns = rhs_leaf.shape[1:]
        picks = coupling.shape[1]
        wide = rhs_sep.shape[0]
        deep = sep_inv.shape[0]
        rows = wide * groups
        half = columns // 2
        skips = tuple(g * wide // (2 * deep) for g in range(groups))
        vmem = pl.BlockSpec(memory_space=pltpu.VMEM)
        anywhere = pl.BlockSpec(memory_space=pl.ANY)
        dma = pltpu.SemaphoreType.DMA
        out, sol = pl.pallas_call(
            functools.partial(kernel, groups, chips, skips),
            out_shape=(
                jax.ShapeDtypeStruct((columns, width), F32),
                jax.ShapeDtypeStruct((columns, wide), F32),
            ),
            in_specs=[vmem, anywhere, anywhere, anywhere, vmem, vmem, anywhere],
            out_specs=(vmem, vmem),
            scratch_shapes=[
                pltpu.VMEM((3, 2, width, width), BF16),
                pltpu.VMEM((2, width, width), BF16),
                pltpu.VMEM((2, picks, width), BF16),
                pltpu.VMEM((2, half, width), F32),
                pltpu.VMEM((3, half, width), F32),
                pltpu.VMEM((half, width), F32),
                pltpu.VMEM((half, picks), F32),
                pltpu.VMEM((half, picks), F32),
                pltpu.VMEM((groups, half, picks), F32),
                pltpu.VMEM((groups, half, wide), F32),
                pltpu.VMEM((groups, 1, picks), jnp.int32),
                pltpu.VMEM((groups, 2, chips, deep, wide), BF16),
                pltpu.VMEM((groups, rows, picks), BF16),
                pltpu.VMEM((2, half, chips * deep), F32),
                pltpu.VMEM((half, rows), F32),
                pltpu.VMEM((half, picks), F32),
                pltpu.VMEM((2, half, wide), F32),
                pltpu.VMEM((half, width), F32),
                pltpu.VMEM((half, width), F32),
                pltpu.VMEM((2, half, width), F32),
                pltpu.VMEM((2, half, width), F32),
                dma((3,)), dma((4,)), dma((4,)), dma, dma, dma, dma, dma, dma,
                dma((groups,)), dma((groups,)), dma((groups,)), dma((groups,)),
                dma((groups,)), dma((groups,)), dma((groups,)), dma((groups,)),
                dma((groups,)), dma((groups,)),
                dma((chips,)), dma, dma((chips,)), dma, dma, dma, dma, dma,
            ],
            compiler_params=pltpu.CompilerParams(
                collective_id=0, has_side_effects=True, vmem_limit_bytes=40 * 1024 * 1024
            ),
        )(
            rhs_leaf[0].T, diag_inv[0, 0], sub_block[0, 0], coupling[0],
            update_rows, rhs_sep.T, sep_inv,
        )
        return out.T[None], sol.T

    return jax.shard_map(
        shards,
        mesh=mesh,
        in_specs=(
            P("leaf", "front", None),
            P("leaf", "front", None, None),
            P("leaf", "front", None, None),
            P("leaf", None, "front"),
            P("leaf", None),
            P("leaf", None),
            P("front", "leaf"),
        ),
        out_specs=(P("leaf", "front", None), P("leaf", None)),
        check_vma=False,
    )
```

```python
import functools

import jax
import jax.numpy as jnp
from jax import lax
from jax.experimental import pallas as pl
from jax.experimental.pallas import tpu as pltpu
from jax.sharding import PartitionSpec as P

MESH = pl.DeviceIdType.MESH
F32 = jnp.float32
BF16 = jnp.bfloat16


def halves(x):
    head = x.astype(BF16)
    rest = (x - head.astype(F32)).astype(BF16)
    return jnp.concatenate([head, rest], axis=0)


def joined(both):
    rows = both.shape[0] // 2
    return both[:rows] + both[rows:]


def times(x, w):
    return joined(jnp.dot(halves(x), w, preferred_element_type=F32))


def times_t(x, w):
    dims = (((1,), (1,)), ((), ()))
    return joined(lax.dot_general(halves(x), w, dims, preferred_element_type=F32))


def dot(a, b):
    return jnp.dot(a, b, preferred_element_type=F32)


def dot_t(a, b):
    return lax.dot_general(a, b, (((1,), (1,)), ((), ())), preferred_element_type=F32)


def split(x):
    head = x.astype(BF16)
    return head, (x - head.astype(F32)).astype(BF16)


def through(x, w, multiply):
    head, rest = w
    both = halves(x)
    return joined(multiply(both, head)) + multiply(both[: x.shape[0]], rest)


def kernel(
    groups, chips, skips,
    r_ref, d_ref, b_ref, c_ref, idx_ref, rs_ref, sp_ref,
    out_ref, sol_ref,
    fac, maps, later, tbuf, turned_out, rbuf, ybuf, yin, uin, uout, ubuf, rsbuf, idxbuf, sepbuf, sel, ssep, solt,
    zbuf, solbuf, vin, vout, xs, obuf,
    loc_s, swap_s, swap_r, y_s, y_r, u_s, u_r, v_s, v_r,
    ux_s, ux_r, rs_s, rs_r, id_s, id_r, sep_s, sep_r, fwd_s, fwd_r,
    m_s, m_r, mf_s, mf_r, t_s, t_r,
    z_s, z_r, so_s, so_r, x_s, x_r, sx_s, sx_r,
):
    plane = lax.axis_index("leaf")
    front = lax.axis_index("front")
    chip = front // 2
    core = front % 2
    other = 1 - core
    last = chips - 1
    is_last = chip == last
    sibling = (plane, chip * 2 + other)
    half = rbuf.shape[1]
    wide = solt.shape[1] // groups
    deep = sepbuf.shape[3]

    def remote(src, dst, send, recv, to):
        return pltpu.make_async_remote_copy(
            src_ref=src, dst_ref=dst, send_sem=send, recv_sem=recv, device_id=to, device_id_type=MESH
        )

    barrier = pltpu.get_barrier_semaphore()

    def greet(to):
        pl.semaphore_signal(barrier, inc=1, device_id=to, device_id_type=MESH)

    greet(sibling)

    @pl.when(is_last)
    def _():
        for g in range(groups):
            for c in range(chips):
                if c < last:
                    greet((g, c * 2 + core))
                else:
                    @pl.when(plane != g)
                    def _(g=g, c=c):
                        greet((g, c * 2 + core))

    @pl.when(jnp.logical_not(is_last))
    def _():
        for g in range(groups):
            greet((g, last * 2 + core))

        for c in range(last):
            @pl.when(chip != c)
            def _(c=c):
                greet((plane, c * 2 + core))

    pl.semaphore_wait(barrier, jnp.where(is_last, groups * chips, groups + last))

    swaps = []
    locals_ = []
    for i, ref in enumerate((b_ref, d_ref, c_ref)):
        copy = remote(ref, fac.at[i, core], swap_s.at[i], swap_r.at[i], sibling)
        copy.start()
        swaps.append(copy)
        copy = pltpu.make_async_copy(ref, fac.at[i, core], loc_s.at[i])
        copy.start()
        locals_.append(copy)
    mine_rows = pl.ds(pl.multiple_of(core * half, half), half)
    other_rows = pl.ds(pl.multiple_of(other * half, half), half)
    copy = pltpu.make_async_copy(r_ref.at[mine_rows], rbuf.at[core], loc_s.at[3])
    copy.start()
    locals_.append(copy)
    copy = remote(r_ref.at[other_rows], rbuf.at[core], swap_s.at[3], swap_r.at[3], sibling)
    copy.start()
    swaps.append(copy)

    def sep_copies(g):
        return remote(
            sp_ref, sepbuf.at[plane, core, chip], sep_s.at[g], sep_r.at[plane], (g, last * 2 + core)
        )

    useful = chip >= (plane * wide) // (2 * deep)
    for g in range(groups):
        mine = jnp.logical_and(is_last, plane == g)

        @pl.when(jnp.logical_and(useful, jnp.logical_not(mine)))
        def _(g=g):
            sep_copies(g).start()

        @pl.when(mine)
        def _(g=g):
            pltpu.make_async_copy(sp_ref, sepbuf.at[g, core, last], sep_r.at[g]).start()

    def peers(action):
        for g in range(groups):
            @pl.when(plane != g)
            def _(g=g):
                action(g, (g, last * 2 + core))

    @pl.when(is_last)
    def _():
        pltpu.make_async_copy(rs_ref.at[mine_rows], rsbuf.at[plane], loc_s.at[4]).start()
        pltpu.make_async_copy(idx_ref, idxbuf.at[plane], loc_s.at[5]).start()

        def give(g, to):
            remote(rs_ref.at[mine_rows], rsbuf.at[plane], rs_s.at[g], rs_r.at[plane], to).start()
            remote(idx_ref, idxbuf.at[plane], id_s.at[g], id_r.at[plane], to).start()

        peers(give)

    for copy in locals_:
        copy.wait()
    for copy in swaps:
        copy.wait_recv()

    onward = (plane, jnp.minimum(front + 2, last * 2 + core))
    y_copy = remote(ybuf.at[2], yin, y_s, y_r, onward)
    u_copy = remote(uout, uin, u_s, u_r, onward)
    u_copies = []
    for step in range(1, groups):
        g = lax.rem(plane + step, groups)
        u_copies.append(
            remote(uout, ubuf.at[plane], ux_s.at[step - 1], ux_r.at[plane], (g, last * 2 + core))
        )

    own_first = times_t(rbuf[0], fac[1, 0])
    own_second = times_t(rbuf[1] - times_t(own_first, fac[0, 1]), fac[1, 1])

    @pl.when(chip == 0)
    def _():
        yin[...] = jnp.zeros_like(yin)
        uin[...] = jnp.zeros_like(uin)
        ybuf[2] = own_second
        y_copy.start()

    own_update = times_t(own_first, fac[2, 0]) + times_t(own_second, fac[2, 1])
    early = split(dot(fac[1, 0], fac[0, 0]))
    late = split(dot(fac[1, 1], fac[0, 1]))
    whole = split(dot(late[0], early[0]) + (dot(late[1], early[0]) + dot(late[0], early[1])))
    seen = split(
        dot(fac[2, 1], whole[0]) - dot(fac[2, 0], early[0])
        + (dot(fac[2, 1], whole[1]) - dot(fac[2, 0], early[1]))
    )
    for part in range(2):
        maps[part, 0] = whole[part]
        maps[part, 1] = seen[part]

    def map_copy(c, to):
        return remote(maps.at[core], later.at[c - 1, core], m_s.at[to], m_r.at[c - 1], (plane, to * 2 + core))

    def turned_copy(c, to):
        return remote(turned_out, tbuf.at[c - 1], t_s.at[to], t_r.at[c - 1], (plane, to * 2 + core))

    def map_onward(c, k):
        part = later.at[c - 1, k]
        return remote(part, part, mf_s.at[c - 1], mf_r.at[c - 1], sibling)

    def to_earlier(action):
        for c in range(1, last):
            @pl.when(chip == c)
            def _(c=c):
                for to in reversed(range(c)):
                    action(c, to)

    def from_later(action):
        for c in reversed(range(1, last)):
            @pl.when(chip < c)
            def _(c=c):
                action(c)

    to_earlier(lambda c, to: map_copy(c, to).start())

    @pl.when(is_last)
    def _():
        def take(g, to):
            remote(idx_ref, idxbuf.at[g], id_s.at[g], id_r.at[g], to).wait_recv()
            remote(rs_ref.at[mine_rows], rsbuf.at[g], rs_s.at[g], rs_r.at[g], to).wait_recv()

        peers(take)
        pltpu.make_async_copy(rs_ref.at[mine_rows], rsbuf.at[plane], loc_s.at[4]).wait()
        pltpu.make_async_copy(idx_ref, idxbuf.at[plane], loc_s.at[5]).wait()
        for g in range(groups):
            rows = lax.broadcasted_iota(jnp.int32, sel.shape[1:], 0)
            sel[g] = (rows == idxbuf[g]).astype(F32).astype(BF16)
        for g in range(groups):
            part = sepbuf.at[g, core, pl.ds(skips[g], chips - skips[g])]
            pltpu.make_async_copy(part, part, sep_r.at[g]).wait()
            remote(part, part, fwd_s.at[g], fwd_r.at[g], sibling).start()

    @pl.when(chip > 0)
    def _():
        y_copy.wait_recv()

    heard = yin[...]
    second = own_second + through(heard, whole, dot_t)
    ybuf[1] = second

    @pl.when(jnp.logical_and(chip > 0, jnp.logical_not(is_last)))
    def _():
        ybuf[2] = second
        y_copy.start()

    update = own_update + through(heard, seen, dot_t)

    @pl.when(chip > 0)
    def _():
        u_copy.wait_recv()

    uout[...] = update + uin[...]

    @pl.when(jnp.logical_not(is_last))
    def _():
        u_copy.start()

    @pl.when(is_last)
    def _():
        for step in range(1, groups):
            u_copies[step - 1].start()

    first = own_first - times_t(times_t(heard, fac[0, 0]), fac[1, 0])
    ybuf[0] = first
    turned = times(times(first, fac[1, 0]), fac[0, 0]) - through(second, whole, dot)
    turned_out[...] = turned
    to_earlier(lambda c, to: turned_copy(c, to).start())

    def pass_on(c):
        map_copy(c, 0).wait_recv()
        map_onward(c, core).start()

    from_later(pass_on)

    z_copies = [
        remote(zbuf, zbuf, z_s.at[c], z_r, (plane, c * 2 + core)) for c in range(last)
    ]
    v_copies = [
        remote(vout, vin, v_s.at[c], v_r, (plane, c * 2 + core)) for c in range(last)
    ]
    so_copies = [
        remote(solbuf.at[core], solbuf.at[core], so_s.at[c], so_r, (plane, c * 2 + core))
        for c in range(last)
    ]

    @pl.when(is_last)
    def _():
        total = times_t(uout[...], sel[plane])
        for g in range(groups):
            part = sepbuf.at[g, other, pl.ds(skips[g], chips - skips[g])]
            remote(part, part, fwd_s.at[g], fwd_r.at[g], sibling).wait_recv()
        for step in range(1, groups):
            g = lax.rem(plane + step, groups)
            remote(uout, ubuf.at[g], ux_s.at[step - 1], ux_r.at[g], (g, last * 2 + core)).wait_recv()
            total = total + times_t(ubuf[g], sel[g])
        ssep[...] = jnp.zeros_like(ssep)
        for g in range(groups):
            part = halves(rsbuf[g] - total[:, g * wide : (g + 1) * wide])
            for k in range(2):
                block = sepbuf[g, k, skips[g] :].reshape((chips - skips[g]) * deep, wide)
                ssep[k, :, skips[g] * deep :] += joined(
                    lax.dot_general(part, block, (((1,), (1,)), ((), ())), preferred_element_type=F32)
                )
        for g in range(groups):
            part = 0
            for k in range(2):
                block = sepbuf[g, k, skips[g] :].reshape((chips - skips[g]) * deep, wide)
                part = part + times(ssep[k, :, skips[g] * deep :], block)
            solt[:, g * wide : (g + 1) * wide] = part

            @pl.when(plane == g)
            def _(part=part):
                solbuf[core] = part

        found = times(solt[...], sel[plane])
        zbuf[...] = found
        for copy in z_copies:
            copy.start()
        vout[...] = turned + through(found, seen, dot)
        vin[...] = jnp.zeros_like(vin)
        for copy in v_copies:
            copy.start()
        for copy in so_copies:
            copy.start()

    @pl.when(jnp.logical_not(is_last))
    def _():
        z_copies[0].wait_recv()

    picked = halves(zbuf[...])
    a_first = ybuf[0] - joined(jnp.dot(picked, fac[2, 0], preferred_element_type=F32))
    a_second = ybuf[1] - joined(jnp.dot(picked, fac[2, 1], preferred_element_type=F32))

    @pl.when(jnp.logical_not(is_last))
    def _():
        v_copies[0].wait_recv()

    def step_back(c):
        turned_copy(c, 0).wait_recv()
        map_onward(c, other).wait_recv()
        moved = through(zbuf[...], (later[c - 1, 0, 1], later[c - 1, 1, 1]), dot)
        vin[...] = tbuf[c - 1] + moved + through(vin[...], (later[c - 1, 0, 0], later[c - 1, 1, 0]), dot)

    from_later(step_back)

    x_second = times(a_second - vin[...], fac[1, 1])
    x_first = times(a_first - times(x_second, fac[0, 1]), fac[1, 0])
    xs[0] = x_first
    xs[1] = x_second
    obuf[core] = xs[core]
    x_copy = remote(xs.at[other], obuf.at[core], x_s, x_r, sibling)
    x_copy.start()

    @pl.when(jnp.logical_not(is_last))
    def _():
        so_copies[0].wait_recv()

    sx_copy = remote(solbuf.at[core], solbuf.at[core], sx_s, sx_r, sibling)
    sx_copy.start()
    x_copy.wait_recv()
    for k in range(2):
        out_ref[k * half : (k + 1) * half] = obuf[k]
    sx_copy.wait_recv()
    for k in range(2):
        sol_ref[k * half : (k + 1) * half] = solbuf[k]

    for copy in swaps:
        copy.wait_send()
    for g in range(groups):
        mine = jnp.logical_and(is_last, plane == g)

        @pl.when(jnp.logical_and(useful, jnp.logical_not(mine)))
        def _(g=g):
            sep_copies(g).wait_send()

    @pl.when(jnp.logical_not(is_last))
    def _():
        y_copy.wait_send()
        u_copy.wait_send()

    to_earlier(lambda c, to: map_copy(c, to).wait_send())
    to_earlier(lambda c, to: turned_copy(c, to).wait_send())
    from_later(lambda c: map_onward(c, core).wait_send())

    @pl.when(is_last)
    def _():
        def sent(g, to):
            remote(rs_ref.at[mine_rows], rsbuf.at[plane], rs_s.at[g], rs_r.at[plane], to).wait_send()
            remote(idx_ref, idxbuf.at[plane], id_s.at[g], id_r.at[plane], to).wait_send()

        peers(sent)
        for copy in u_copies:
            copy.wait_send()
        for g in range(groups):
            part = sepbuf.at[g, core, pl.ds(skips[g], chips - skips[g])]
            remote(part, part, fwd_s.at[g], fwd_r.at[g], sibling).wait_send()
        for copy in z_copies:
            copy.wait_send()
        for copy in v_copies + so_copies:
            copy.wait_send()

    x_copy.wait_send()
    sx_copy.wait_send()


def solution(mesh):
    groups, fronts = mesh.shape["leaf"], mesh.shape["front"]
    chips = fronts // 2

    def shards(rhs_leaf, diag_inv, sub_block, coupling, update_rows, rhs_sep, sep_inv):
        width, columns = rhs_leaf.shape[1:]
        picks = coupling.shape[1]
        wide = rhs_sep.shape[0]
        deep = sep_inv.shape[0]
        rows = wide * groups
        half = columns // 2
        skips = tuple(g * wide // (2 * deep) for g in range(groups))
        vmem = pl.BlockSpec(memory_space=pltpu.VMEM)
        hbm = pl.BlockSpec(memory_space=pltpu.HBM)
        dma = pltpu.SemaphoreType.DMA
        out, sol = pl.pallas_call(
            functools.partial(kernel, groups, chips, skips),
            out_shape=(
                jax.ShapeDtypeStruct((columns, width), F32),
                jax.ShapeDtypeStruct((columns, wide), F32),
            ),
            in_specs=[hbm] * 7,
            out_specs=(vmem, vmem),
            scratch_shapes=[
                pltpu.VMEM((3, 2, width, width), BF16),
                pltpu.VMEM((2, 2, width, width), BF16),
                pltpu.VMEM((chips - 2, 2, 2, width, width), BF16),
                pltpu.VMEM((chips - 2, half, width), F32),
                pltpu.VMEM((half, width), F32),
                pltpu.VMEM((2, half, width), F32),
                pltpu.VMEM((3, half, width), F32),
                pltpu.VMEM((half, width), F32),
                pltpu.VMEM((half, picks), F32),
                pltpu.VMEM((half, picks), F32),
                pltpu.VMEM((groups, half, picks), F32),
                pltpu.VMEM((groups, half, wide), F32),
                pltpu.VMEM((groups, 1, picks), jnp.int32),
                pltpu.VMEM((groups, 2, chips, deep, wide), BF16),
                pltpu.VMEM((groups, rows, picks), BF16),
                pltpu.VMEM((2, half, chips * deep), F32),
                pltpu.VMEM((half, rows), F32),
                pltpu.VMEM((half, picks), F32),
                pltpu.VMEM((2, half, wide), F32),
                pltpu.VMEM((half, width), F32),
                pltpu.VMEM((half, width), F32),
                pltpu.VMEM((2, half, width), F32),
                pltpu.VMEM((2, half, width), F32),
                dma((6,)), dma((4,)), dma((4,)), dma, dma, dma, dma, dma((chips,)), dma,
                dma((groups,)), dma((groups,)), dma((groups,)), dma((groups,)),
                dma((groups,)), dma((groups,)), dma((groups,)), dma((groups,)),
                dma((groups,)), dma((groups,)),
                dma((chips,)), dma((chips,)), dma((chips,)), dma((chips,)), dma((chips,)), dma((chips,)),
                dma((chips,)), dma, dma((chips,)), dma, dma, dma, dma, dma,
            ],
            compiler_params=pltpu.CompilerParams(
                collective_id=0, has_side_effects=True, vmem_limit_bytes=64 * 1024 * 1024
            ),
        )(
            rhs_leaf[0].T, diag_inv[0, 0], sub_block[0, 0], coupling[0],
            update_rows, rhs_sep.T, sep_inv,
        )
        return out.T[None], sol.T

    return jax.shard_map(
        shards,
        mesh=mesh,
        in_specs=(
            P("leaf", "front", None),
            P("leaf", "front", None, None),
            P("leaf", "front", None, None),
            P("leaf", None, "front"),
            P("leaf", None),
            P("leaf", None),
            P("front", "leaf"),
        ),
        out_specs=(P("leaf", "front", None), P("leaf", None)),
        check_vma=False,
    )
```

```python
import functools

import jax
import jax.numpy as jnp
from jax import lax
from jax.experimental import pallas as pl
from jax.experimental.pallas import tpu as pltpu
from jax.sharding import PartitionSpec as P

MESH = pl.DeviceIdType.MESH
F32 = jnp.float32
BF16 = jnp.bfloat16


def halves(x):
    head = x.astype(BF16)
    rest = (x - head.astype(F32)).astype(BF16)
    return jnp.concatenate([head, rest], axis=0)


def joined(both):
    rows = both.shape[0] // 2
    return both[:rows] + both[rows:]


def times(x, w):
    return joined(jnp.dot(halves(x), w, preferred_element_type=F32))


def times_t(x, w):
    dims = (((1,), (1,)), ((), ()))
    return joined(lax.dot_general(halves(x), w, dims, preferred_element_type=F32))


def dot(a, b):
    return jnp.dot(a, b, preferred_element_type=F32)


def dot_t(a, b):
    return lax.dot_general(a, b, (((1,), (1,)), ((), ())), preferred_element_type=F32)


def split(x):
    head = x.astype(BF16)
    return head, (x - head.astype(F32)).astype(BF16)


def through(x, w, multiply):
    head, rest = w
    both = halves(x)
    return joined(multiply(both, head)) + multiply(both[: x.shape[0]], rest)


def kernel(
    groups, chips, skips,
    r_ref, d_ref, b_ref, c_ref, idx_ref, rs_ref, sp_ref,
    out_ref, sol_ref,
    fac, maps, later, tbuf, turned_out, rbuf, ybuf, yin, uin, uout, ubuf, rsbuf, idxbuf, sepbuf, sel, ssep, solt,
    zbuf, solbuf, vin, vout, xs, obuf,
    loc_s, swap_s, swap_r, y_s, y_r, u_s, u_r, v_s, v_r,
    ux_s, ux_r, rs_s, rs_r, id_s, id_r, sep_s, sep_r, fwd_s, fwd_r,
    m_s, m_r, mf_s, mf_r, t_s, t_r,
    z_s, z_r, so_s, so_r, x_s, x_r, sx_s, sx_r,
):
    plane = lax.axis_index("leaf")
    front = lax.axis_index("front")
    chip = front // 2
    core = front % 2
    other = 1 - core
    last = chips - 1
    is_last = chip == last
    sibling = (plane, chip * 2 + other)
    half = rbuf.shape[1]
    wide = solt.shape[1] // groups
    deep = sepbuf.shape[3]

    def remote(src, dst, send, recv, to):
        return pltpu.make_async_remote_copy(
            src_ref=src, dst_ref=dst, send_sem=send, recv_sem=recv, device_id=to, device_id_type=MESH
        )

    barrier = pltpu.get_barrier_semaphore()

    def greet(to):
        pl.semaphore_signal(barrier, inc=1, device_id=to, device_id_type=MESH)

    greet(sibling)

    @pl.when(is_last)
    def _():
        for g in range(groups):
            for c in range(chips):
                if c < last:
                    greet((g, c * 2 + core))
                else:
                    @pl.when(plane != g)
                    def _(g=g, c=c):
                        greet((g, c * 2 + core))

    @pl.when(jnp.logical_not(is_last))
    def _():
        for g in range(groups):
            greet((g, last * 2 + core))

        for c in range(last):
            @pl.when(chip != c)
            def _(c=c):
                greet((plane, c * 2 + core))

    pl.semaphore_wait(barrier, jnp.where(is_last, groups * chips, groups + last))

    swaps = []
    locals_ = []
    for i, ref in enumerate((b_ref, d_ref, c_ref)):
        copy = remote(ref, fac.at[i, core], swap_s.at[i], swap_r.at[i], sibling)
        copy.start()
        swaps.append(copy)
        copy = pltpu.make_async_copy(ref, fac.at[i, core], loc_s.at[i])
        copy.start()
        locals_.append(copy)
    mine_rows = pl.ds(pl.multiple_of(core * half, half), half)
    other_rows = pl.ds(pl.multiple_of(other * half, half), half)
    copy = pltpu.make_async_copy(r_ref.at[mine_rows], rbuf.at[core], loc_s.at[3])
    copy.start()
    locals_.append(copy)
    copy = remote(r_ref.at[other_rows], rbuf.at[core], swap_s.at[3], swap_r.at[3], sibling)
    copy.start()
    swaps.append(copy)

    def sep_copies(g):
        return remote(
            sp_ref, sepbuf.at[plane, core, chip], sep_s.at[g], sep_r.at[plane], (g, last * 2 + core)
        )

    useful = chip >= (plane * wide) // (2 * deep)
    for g in range(groups):
        mine = jnp.logical_and(is_last, plane == g)

        @pl.when(jnp.logical_and(useful, jnp.logical_not(mine)))
        def _(g=g):
            sep_copies(g).start()

        @pl.when(mine)
        def _(g=g):
            pltpu.make_async_copy(sp_ref, sepbuf.at[g, core, last], sep_r.at[g]).start()

    def peers(action):
        for g in range(groups):
            @pl.when(plane != g)
            def _(g=g):
                action(g, (g, last * 2 + core))

    @pl.when(is_last)
    def _():
        pltpu.make_async_copy(rs_ref.at[mine_rows], rsbuf.at[plane], loc_s.at[4]).start()
        pltpu.make_async_copy(idx_ref, idxbuf.at[plane], loc_s.at[5]).start()

        def give(g, to):
            remote(rs_ref.at[mine_rows], rsbuf.at[plane], rs_s.at[g], rs_r.at[plane], to).start()
            remote(idx_ref, idxbuf.at[plane], id_s.at[g], id_r.at[plane], to).start()

        peers(give)

    for copy in locals_:
        copy.wait()
    for copy in swaps:
        copy.wait_recv()

    onward = (plane, jnp.minimum(front + 2, last * 2 + core))
    y_copy = remote(ybuf.at[2], yin, y_s, y_r, onward)
    u_copy = remote(uout, uin, u_s, u_r, onward)
    u_copies = []
    for step in range(1, groups):
        g = lax.rem(plane + step, groups)
        u_copies.append(
            remote(uout, ubuf.at[plane], ux_s.at[step - 1], ux_r.at[plane], (g, last * 2 + core))
        )

    own_first = times_t(rbuf[0], fac[1, 0])
    own_second = times_t(rbuf[1] - times_t(own_first, fac[0, 1]), fac[1, 1])

    @pl.when(chip == 0)
    def _():
        yin[...] = jnp.zeros_like(yin)
        uin[...] = jnp.zeros_like(uin)
        ybuf[2] = own_second
        y_copy.start()

    own_update = times_t(own_first, fac[2, 0]) + times_t(own_second, fac[2, 1])
    early = split(dot(fac[1, 0], fac[0, 0]))
    late = split(dot(fac[1, 1], fac[0, 1]))
    whole = split(dot(late[0], early[0]) + (dot(late[1], early[0]) + dot(late[0], early[1])))
    seen = split(
        dot(fac[2, 1], whole[0]) - dot(fac[2, 0], early[0])
        + (dot(fac[2, 1], whole[1]) - dot(fac[2, 0], early[1]))
    )
    for part in range(2):
        maps[part, 0] = whole[part]
        maps[part, 1] = seen[part]

    def map_copy(c, to):
        return remote(maps.at[core], later.at[c - 1, core], m_s.at[to], m_r.at[c - 1], (plane, to * 2 + core))

    def turned_copy(c, to):
        return remote(turned_out, tbuf.at[c - 1], t_s.at[to], t_r.at[c - 1], (plane, to * 2 + core))

    def map_onward(c, k):
        part = later.at[c - 1, k]
        return remote(part, part, mf_s.at[c - 1], mf_r.at[c - 1], sibling)

    def to_earlier(action):
        for c in range(1, last):
            @pl.when(chip == c)
            def _(c=c):
                for to in reversed(range(c)):
                    action(c, to)

    def from_later(action):
        for c in reversed(range(1, last)):
            @pl.when(chip < c)
            def _(c=c):
                action(c)

    @pl.when(is_last)
    def _():
        def take(g, to):
            remote(idx_ref, idxbuf.at[g], id_s.at[g], id_r.at[g], to).wait_recv()
            remote(rs_ref.at[mine_rows], rsbuf.at[g], rs_s.at[g], rs_r.at[g], to).wait_recv()

        peers(take)
        pltpu.make_async_copy(rs_ref.at[mine_rows], rsbuf.at[plane], loc_s.at[4]).wait()
        pltpu.make_async_copy(idx_ref, idxbuf.at[plane], loc_s.at[5]).wait()
        for g in range(groups):
            rows = lax.broadcasted_iota(jnp.int32, sel.shape[1:], 0)
            sel[g] = (rows == idxbuf[g]).astype(F32).astype(BF16)
        for g in range(groups):
            part = sepbuf.at[g, core, pl.ds(skips[g], chips - skips[g])]
            pltpu.make_async_copy(part, part, sep_r.at[g]).wait()
            remote(part, part, fwd_s.at[g], fwd_r.at[g], sibling).start()

    @pl.when(chip > 0)
    def _():
        y_copy.wait_recv()

    heard = yin[...]
    second = own_second + through(heard, whole, dot_t)
    ybuf[1] = second

    @pl.when(jnp.logical_and(chip > 0, jnp.logical_not(is_last)))
    def _():
        ybuf[2] = second
        y_copy.start()

    update = own_update + through(heard, seen, dot_t)

    @pl.when(chip > 0)
    def _():
        u_copy.wait_recv()

    uout[...] = update + uin[...]

    @pl.when(jnp.logical_not(is_last))
    def _():
        u_copy.start()

    @pl.when(is_last)
    def _():
        for step in range(1, groups):
            u_copies[step - 1].start()

    first = own_first - times_t(times_t(heard, fac[0, 0]), fac[1, 0])
    ybuf[0] = first
    turned = times(times(first, fac[1, 0]), fac[0, 0]) - through(second, whole, dot)
    turned_out[...] = turned
    to_earlier(lambda c, to: map_copy(c, to).start())
    to_earlier(lambda c, to: turned_copy(c, to).start())

    def pass_on(c):
        map_copy(c, 0).wait_recv()
        map_onward(c, core).start()

    from_later(pass_on)

    z_copies = [
        remote(zbuf, zbuf, z_s.at[c], z_r, (plane, c * 2 + core)) for c in range(last)
    ]
    v_copies = [
        remote(vout, vin, v_s.at[c], v_r, (plane, c * 2 + core)) for c in range(last)
    ]
    so_copies = [
        remote(solbuf.at[core], solbuf.at[core], so_s.at[c], so_r, (plane, c * 2 + core))
        for c in range(last)
    ]

    @pl.when(is_last)
    def _():
        total = times_t(uout[...], sel[plane])
        for g in range(groups):
            part = sepbuf.at[g, other, pl.ds(skips[g], chips - skips[g])]
            remote(part, part, fwd_s.at[g], fwd_r.at[g], sibling).wait_recv()
        for step in range(1, groups):
            g = lax.rem(plane + step, groups)
            remote(uout, ubuf.at[g], ux_s.at[step - 1], ux_r.at[g], (g, last * 2 + core)).wait_recv()
            total = total + times_t(ubuf[g], sel[g])
        ssep[...] = jnp.zeros_like(ssep)
        for g in range(groups):
            part = halves(rsbuf[g] - total[:, g * wide : (g + 1) * wide])
            for k in range(2):
                block = sepbuf[g, k, skips[g] :].reshape((chips - skips[g]) * deep, wide)
                ssep[k, :, skips[g] * deep :] += joined(
                    lax.dot_general(part, block, (((1,), (1,)), ((), ())), preferred_element_type=F32)
                )
        for g in range(groups):
            part = 0
            for k in range(2):
                block = sepbuf[g, k, skips[g] :].reshape((chips - skips[g]) * deep, wide)
                part = part + times(ssep[k, :, skips[g] * deep :], block)
            solt[:, g * wide : (g + 1) * wide] = part

            @pl.when(plane == g)
            def _(part=part):
                solbuf[core] = part

        found = times(solt[...], sel[plane])
        zbuf[...] = found
        for copy in z_copies:
            copy.start()
        vout[...] = turned + through(found, seen, dot)
        vin[...] = jnp.zeros_like(vin)
        for copy in v_copies:
            copy.start()
        for copy in so_copies:
            copy.start()

    @pl.when(jnp.logical_not(is_last))
    def _():
        z_copies[0].wait_recv()

    picked = halves(zbuf[...])
    a_first = ybuf[0] - joined(jnp.dot(picked, fac[2, 0], preferred_element_type=F32))
    a_second = ybuf[1] - joined(jnp.dot(picked, fac[2, 1], preferred_element_type=F32))

    @pl.when(jnp.logical_not(is_last))
    def _():
        v_copies[0].wait_recv()

    def step_back(c):
        turned_copy(c, 0).wait_recv()
        map_onward(c, other).wait_recv()
        moved = through(zbuf[...], (later[c - 1, 0, 1], later[c - 1, 1, 1]), dot)
        vin[...] = tbuf[c - 1] + moved + through(vin[...], (later[c - 1, 0, 0], later[c - 1, 1, 0]), dot)

    from_later(step_back)

    x_second = times(a_second - vin[...], fac[1, 1])
    x_first = times(a_first - times(x_second, fac[0, 1]), fac[1, 0])
    xs[0] = x_first
    xs[1] = x_second
    obuf[core] = xs[core]
    x_copy = remote(xs.at[other], obuf.at[core], x_s, x_r, sibling)
    x_copy.start()

    @pl.when(jnp.logical_not(is_last))
    def _():
        so_copies[0].wait_recv()

    sx_copy = remote(solbuf.at[core], solbuf.at[core], sx_s, sx_r, sibling)
    sx_copy.start()
    x_copy.wait_recv()
    for k in range(2):
        out_ref[k * half : (k + 1) * half] = obuf[k]
    sx_copy.wait_recv()
    for k in range(2):
        sol_ref[k * half : (k + 1) * half] = solbuf[k]

    for copy in swaps:
        copy.wait_send()
    for g in range(groups):
        mine = jnp.logical_and(is_last, plane == g)

        @pl.when(jnp.logical_and(useful, jnp.logical_not(mine)))
        def _(g=g):
            sep_copies(g).wait_send()

    @pl.when(jnp.logical_not(is_last))
    def _():
        y_copy.wait_send()
        u_copy.wait_send()

    to_earlier(lambda c, to: map_copy(c, to).wait_send())
    to_earlier(lambda c, to: turned_copy(c, to).wait_send())
    from_later(lambda c: map_onward(c, core).wait_send())

    @pl.when(is_last)
    def _():
        def sent(g, to):
            remote(rs_ref.at[mine_rows], rsbuf.at[plane], rs_s.at[g], rs_r.at[plane], to).wait_send()
            remote(idx_ref, idxbuf.at[plane], id_s.at[g], id_r.at[plane], to).wait_send()

        peers(sent)
        for copy in u_copies:
            copy.wait_send()
        for g in range(groups):
            part = sepbuf.at[g, core, pl.ds(skips[g], chips - skips[g])]
            remote(part, part, fwd_s.at[g], fwd_r.at[g], sibling).wait_send()
        for copy in z_copies:
            copy.wait_send()
        for copy in v_copies + so_copies:
            copy.wait_send()

    x_copy.wait_send()
    sx_copy.wait_send()


def solution(mesh):
    groups, fronts = mesh.shape["leaf"], mesh.shape["front"]
    chips = fronts // 2

    def shards(rhs_leaf, diag_inv, sub_block, coupling, update_rows, rhs_sep, sep_inv):
        width, columns = rhs_leaf.shape[1:]
        picks = coupling.shape[1]
        wide = rhs_sep.shape[0]
        deep = sep_inv.shape[0]
        rows = wide * groups
        half = columns // 2
        skips = tuple(g * wide // (2 * deep) for g in range(groups))
        vmem = pl.BlockSpec(memory_space=pltpu.VMEM)
        hbm = pl.BlockSpec(memory_space=pltpu.HBM)
        dma = pltpu.SemaphoreType.DMA
        out, sol = pl.pallas_call(
            functools.partial(kernel, groups, chips, skips),
            out_shape=(
                jax.ShapeDtypeStruct((columns, width), F32),
                jax.ShapeDtypeStruct((columns, wide), F32),
            ),
            in_specs=[hbm] * 7,
            out_specs=(vmem, vmem),
            scratch_shapes=[
                pltpu.VMEM((3, 2, width, width), BF16),
                pltpu.VMEM((2, 2, width, width), BF16),
                pltpu.VMEM((chips - 2, 2, 2, width, width), BF16),
                pltpu.VMEM((chips - 2, half, width), F32),
                pltpu.VMEM((half, width), F32),
                pltpu.VMEM((2, half, width), F32),
                pltpu.VMEM((3, half, width), F32),
                pltpu.VMEM((half, width), F32),
                pltpu.VMEM((half, picks), F32),
                pltpu.VMEM((half, picks), F32),
                pltpu.VMEM((groups, half, picks), F32),
                pltpu.VMEM((groups, half, wide), F32),
                pltpu.VMEM((groups, 1, picks), jnp.int32),
                pltpu.VMEM((groups, 2, chips, deep, wide), BF16),
                pltpu.VMEM((groups, rows, picks), BF16),
                pltpu.VMEM((2, half, chips * deep), F32),
                pltpu.VMEM((half, rows), F32),
                pltpu.VMEM((half, picks), F32),
                pltpu.VMEM((2, half, wide), F32),
                pltpu.VMEM((half, width), F32),
                pltpu.VMEM((half, width), F32),
                pltpu.VMEM((2, half, width), F32),
                pltpu.VMEM((2, half, width), F32),
                dma((6,)), dma((4,)), dma((4,)), dma, dma, dma, dma, dma((chips,)), dma,
                dma((groups,)), dma((groups,)), dma((groups,)), dma((groups,)),
                dma((groups,)), dma((groups,)), dma((groups,)), dma((groups,)),
                dma((groups,)), dma((groups,)),
                dma((chips,)), dma((chips,)), dma((chips,)), dma((chips,)), dma((chips,)), dma((chips,)),
                dma((chips,)), dma, dma((chips,)), dma, dma, dma, dma, dma,
            ],
            compiler_params=pltpu.CompilerParams(
                collective_id=0, has_side_effects=True, vmem_limit_bytes=64 * 1024 * 1024
            ),
        )(
            rhs_leaf[0].T, diag_inv[0, 0], sub_block[0, 0], coupling[0],
            update_rows, rhs_sep.T, sep_inv,
        )
        return out.T[None], sol.T

    return jax.shard_map(
        shards,
        mesh=mesh,
        in_specs=(
            P("leaf", "front", None),
            P("leaf", "front", None, None),
            P("leaf", "front", None, None),
            P("leaf", None, "front"),
            P("leaf", None),
            P("leaf", None),
            P("front", "leaf"),
        ),
        out_specs=(P("leaf", "front", None), P("leaf", None)),
        check_vma=False,
    )
```

```python
import functools

import jax
import jax.numpy as jnp
from jax import lax
from jax.experimental import pallas as pl
from jax.experimental.pallas import tpu as pltpu
from jax.sharding import PartitionSpec as P

MESH = pl.DeviceIdType.MESH
F32 = jnp.float32
BF16 = jnp.bfloat16


def halves(x):
    head = x.astype(BF16)
    rest = (x - head.astype(F32)).astype(BF16)
    return jnp.concatenate([head, rest], axis=0)


def joined(both):
    rows = both.shape[0] // 2
    return both[:rows] + both[rows:]


def times(x, w):
    return joined(jnp.dot(halves(x), w, preferred_element_type=F32))


def times_t(x, w):
    dims = (((1,), (1,)), ((), ()))
    return joined(lax.dot_general(halves(x), w, dims, preferred_element_type=F32))


def dot(a, b):
    return jnp.dot(a, b, preferred_element_type=F32)


def dot_t(a, b):
    return lax.dot_general(a, b, (((1,), (1,)), ((), ())), preferred_element_type=F32)


def split(x):
    head = x.astype(BF16)
    return head, (x - head.astype(F32)).astype(BF16)


def through(x, w, multiply):
    head, rest = w
    both = halves(x)
    return joined(multiply(both, head)) + multiply(both[: x.shape[0]], rest)


def kernel(
    groups, chips, skips,
    r_ref, d_ref, b_ref, c_ref, idx_ref, rs_ref, sp_ref,
    out_ref, sol_ref,
    fac, maps, later, tbuf, turned_out, rbuf, ybuf, yin, uin, uout, ubuf, rsbuf, idxbuf, sepbuf, sel, ssep, solt,
    zbuf, solbuf, vin, vout, xs, obuf,
    loc_s, swap_s, swap_r, y_s, y_r, u_s, u_r, v_s, v_r,
    ux_s, ux_r, rs_s, rs_r, id_s, id_r, sep_s, sep_r, fwd_s, fwd_r,
    m_s, m_r, mf_s, mf_r, t_s, t_r,
    z_s, z_r, so_s, so_r, x_s, x_r, sx_s, sx_r,
):
    plane = lax.axis_index("leaf")
    front = lax.axis_index("front")
    chip = front // 2
    core = front % 2
    other = 1 - core
    last = chips - 1
    is_last = chip == last
    sibling = (plane, chip * 2 + other)
    half = rbuf.shape[1]
    wide = solt.shape[1] // groups
    deep = sepbuf.shape[3]

    def remote(src, dst, send, recv, to):
        return pltpu.make_async_remote_copy(
            src_ref=src, dst_ref=dst, send_sem=send, recv_sem=recv, device_id=to, device_id_type=MESH
        )

    barrier = pltpu.get_barrier_semaphore()

    def greet(to):
        pl.semaphore_signal(barrier, inc=1, device_id=to, device_id_type=MESH)

    greet(sibling)

    @pl.when(is_last)
    def _():
        for g in range(groups):
            for c in range(chips):
                if c < last:
                    greet((g, c * 2 + core))
                else:
                    @pl.when(plane != g)
                    def _(g=g, c=c):
                        greet((g, c * 2 + core))

    @pl.when(jnp.logical_not(is_last))
    def _():
        for g in range(groups):
            greet((g, last * 2 + core))

        for c in range(last):
            @pl.when(chip != c)
            def _(c=c):
                greet((plane, c * 2 + core))

    mine_rows = pl.ds(pl.multiple_of(core * half, half), half)
    other_rows = pl.ds(pl.multiple_of(other * half, half), half)
    locals_ = [
        pltpu.make_async_copy(ref, fac.at[i, core], loc_s.at[i])
        for i, ref in enumerate((b_ref, d_ref, c_ref))
    ]
    locals_.append(pltpu.make_async_copy(r_ref.at[mine_rows], rbuf.at[core], loc_s.at[3]))
    for copy in locals_:
        copy.start()
    pl.semaphore_wait(barrier, jnp.where(is_last, groups * chips, groups + last))

    swaps = []
    for i, ref in enumerate((b_ref, d_ref, c_ref)):
        copy = remote(ref, fac.at[i, core], swap_s.at[i], swap_r.at[i], sibling)
        copy.start()
        swaps.append(copy)
    copy = remote(r_ref.at[other_rows], rbuf.at[core], swap_s.at[3], swap_r.at[3], sibling)
    copy.start()
    swaps.append(copy)

    def sep_copies(g):
        return remote(
            sp_ref, sepbuf.at[plane, core, chip], sep_s.at[g], sep_r.at[plane], (g, last * 2 + core)
        )

    useful = chip >= (plane * wide) // (2 * deep)
    for g in range(groups):
        mine = jnp.logical_and(is_last, plane == g)

        @pl.when(jnp.logical_and(useful, jnp.logical_not(mine)))
        def _(g=g):
            sep_copies(g).start()

        @pl.when(mine)
        def _(g=g):
            pltpu.make_async_copy(sp_ref, sepbuf.at[g, core, last], sep_r.at[g]).start()

    def peers(action):
        for g in range(groups):
            @pl.when(plane != g)
            def _(g=g):
                action(g, (g, last * 2 + core))

    @pl.when(is_last)
    def _():
        pltpu.make_async_copy(rs_ref.at[mine_rows], rsbuf.at[plane], loc_s.at[4]).start()
        pltpu.make_async_copy(idx_ref, idxbuf.at[plane], loc_s.at[5]).start()

        def give(g, to):
            remote(rs_ref.at[mine_rows], rsbuf.at[plane], rs_s.at[g], rs_r.at[plane], to).start()
            remote(idx_ref, idxbuf.at[plane], id_s.at[g], id_r.at[plane], to).start()

        peers(give)

    for copy in locals_:
        copy.wait()
    for copy in swaps:
        copy.wait_recv()

    onward = (plane, jnp.minimum(front + 2, last * 2 + core))
    y_copy = remote(ybuf.at[2], yin, y_s, y_r, onward)
    u_copy = remote(uout, uin, u_s, u_r, onward)
    u_copies = []
    for step in range(1, groups):
        g = lax.rem(plane + step, groups)
        u_copies.append(
            remote(uout, ubuf.at[plane], ux_s.at[step - 1], ux_r.at[plane], (g, last * 2 + core))
        )

    own_first = times_t(rbuf[0], fac[1, 0])
    own_second = times_t(rbuf[1] - times_t(own_first, fac[0, 1]), fac[1, 1])

    @pl.when(chip == 0)
    def _():
        yin[...] = jnp.zeros_like(yin)
        uin[...] = jnp.zeros_like(uin)
        ybuf[2] = own_second
        y_copy.start()

    own_update = times_t(own_first, fac[2, 0]) + times_t(own_second, fac[2, 1])
    early = split(dot(fac[1, 0], fac[0, 0]))
    late = split(dot(fac[1, 1], fac[0, 1]))
    whole = split(dot(late[0], early[0]) + (dot(late[1], early[0]) + dot(late[0], early[1])))
    seen = split(
        dot(fac[2, 1], whole[0]) - dot(fac[2, 0], early[0])
        + (dot(fac[2, 1], whole[1]) - dot(fac[2, 0], early[1]))
    )
    for part in range(2):
        maps[part, 0] = whole[part]
        maps[part, 1] = seen[part]

    def map_copy(c, to):
        return remote(maps.at[core], later.at[c - 1, core], m_s.at[to], m_r.at[c - 1], (plane, to * 2 + core))

    def turned_copy(c, to):
        return remote(turned_out, tbuf.at[c - 1], t_s.at[to], t_r.at[c - 1], (plane, to * 2 + core))

    def map_onward(c, k):
        part = later.at[c - 1, k]
        return remote(part, part, mf_s.at[c - 1], mf_r.at[c - 1], sibling)

    def to_earlier(action):
        for c in range(1, last):
            @pl.when(chip == c)
            def _(c=c):
                for to in reversed(range(c)):
                    action(c, to)

    def from_later(action):
        for c in reversed(range(1, last)):
            @pl.when(chip < c)
            def _(c=c):
                action(c)

    @pl.when(is_last)
    def _():
        def take(g, to):
            remote(idx_ref, idxbuf.at[g], id_s.at[g], id_r.at[g], to).wait_recv()
            remote(rs_ref.at[mine_rows], rsbuf.at[g], rs_s.at[g], rs_r.at[g], to).wait_recv()

        peers(take)
        pltpu.make_async_copy(rs_ref.at[mine_rows], rsbuf.at[plane], loc_s.at[4]).wait()
        pltpu.make_async_copy(idx_ref, idxbuf.at[plane], loc_s.at[5]).wait()
        for g in range(groups):
            rows = lax.broadcasted_iota(jnp.int32, sel.shape[1:], 0)
            sel[g] = (rows == idxbuf[g]).astype(F32).astype(BF16)

    @pl.when(chip > 0)
    def _():
        y_copy.wait_recv()

    heard = yin[...]
    second = own_second + through(heard, whole, dot_t)
    ybuf[1] = second

    @pl.when(jnp.logical_and(chip > 0, jnp.logical_not(is_last)))
    def _():
        ybuf[2] = second
        y_copy.start()

    update = own_update + through(heard, seen, dot_t)

    @pl.when(chip > 0)
    def _():
        u_copy.wait_recv()

    uout[...] = update + uin[...]

    @pl.when(jnp.logical_not(is_last))
    def _():
        u_copy.start()

    @pl.when(is_last)
    def _():
        for step in range(1, groups):
            u_copies[step - 1].start()
        for g in range(groups):
            part = sepbuf.at[g, core, pl.ds(skips[g], chips - skips[g])]
            pltpu.make_async_copy(part, part, sep_r.at[g]).wait()
            remote(part, part, fwd_s.at[g], fwd_r.at[g], sibling).start()

    first = own_first - times_t(times_t(heard, fac[0, 0]), fac[1, 0])
    ybuf[0] = first
    turned = times(times(first, fac[1, 0]), fac[0, 0]) - through(second, whole, dot)
    turned_out[...] = turned
    to_earlier(lambda c, to: map_copy(c, to).start())
    to_earlier(lambda c, to: turned_copy(c, to).start())

    def pass_on(c):
        map_copy(c, 0).wait_recv()
        map_onward(c, core).start()

    from_later(pass_on)

    z_copies = [
        remote(zbuf, zbuf, z_s.at[c], z_r, (plane, c * 2 + core)) for c in range(last)
    ]
    v_copies = [
        remote(vout, vin, v_s.at[c], v_r, (plane, c * 2 + core)) for c in range(last)
    ]
    so_copies = [
        remote(solbuf.at[core], solbuf.at[core], so_s.at[c], so_r, (plane, c * 2 + core))
        for c in range(last)
    ]

    @pl.when(is_last)
    def _():
        total = times_t(uout[...], sel[plane])
        for g in range(groups):
            part = sepbuf.at[g, other, pl.ds(skips[g], chips - skips[g])]
            remote(part, part, fwd_s.at[g], fwd_r.at[g], sibling).wait_recv()
        for step in range(1, groups):
            g = lax.rem(plane + step, groups)
            remote(uout, ubuf.at[g], ux_s.at[step - 1], ux_r.at[g], (g, last * 2 + core)).wait_recv()
            total = total + times_t(ubuf[g], sel[g])
        ssep[...] = jnp.zeros_like(ssep)
        for g in range(groups):
            part = halves(rsbuf[g] - total[:, g * wide : (g + 1) * wide])
            for k in range(2):
                block = sepbuf[g, k, skips[g] :].reshape((chips - skips[g]) * deep, wide)
                ssep[k, :, skips[g] * deep :] += joined(
                    lax.dot_general(part, block, (((1,), (1,)), ((), ())), preferred_element_type=F32)
                )
        for g in range(groups):
            part = 0
            for k in range(2):
                block = sepbuf[g, k, skips[g] :].reshape((chips - skips[g]) * deep, wide)
                part = part + times(ssep[k, :, skips[g] * deep :], block)
            solt[:, g * wide : (g + 1) * wide] = part

            @pl.when(plane == g)
            def _(part=part):
                solbuf[core] = part

        found = times(solt[...], sel[plane])
        zbuf[...] = found
        for copy in z_copies:
            copy.start()
        vout[...] = turned + through(found, seen, dot)
        vin[...] = jnp.zeros_like(vin)
        for copy in v_copies:
            copy.start()
        for copy in so_copies:
            copy.start()

    @pl.when(jnp.logical_not(is_last))
    def _():
        z_copies[0].wait_recv()

    picked = halves(zbuf[...])
    a_first = ybuf[0] - joined(jnp.dot(picked, fac[2, 0], preferred_element_type=F32))
    a_second = ybuf[1] - joined(jnp.dot(picked, fac[2, 1], preferred_element_type=F32))

    @pl.when(jnp.logical_not(is_last))
    def _():
        v_copies[0].wait_recv()

    def step_back(c):
        turned_copy(c, 0).wait_recv()
        map_onward(c, other).wait_recv()
        moved = through(zbuf[...], (later[c - 1, 0, 1], later[c - 1, 1, 1]), dot)
        vin[...] = tbuf[c - 1] + moved + through(vin[...], (later[c - 1, 0, 0], later[c - 1, 1, 0]), dot)

    from_later(step_back)

    x_second = times(a_second - vin[...], fac[1, 1])
    x_first = times(a_first - times(x_second, fac[0, 1]), fac[1, 0])
    xs[0] = x_first
    xs[1] = x_second
    obuf[core] = xs[core]
    x_copy = remote(xs.at[other], obuf.at[core], x_s, x_r, sibling)
    x_copy.start()

    @pl.when(jnp.logical_not(is_last))
    def _():
        so_copies[0].wait_recv()

    sx_copy = remote(solbuf.at[core], solbuf.at[core], sx_s, sx_r, sibling)
    sx_copy.start()
    x_copy.wait_recv()
    for k in range(2):
        out_ref[k * half : (k + 1) * half] = obuf[k]
    sx_copy.wait_recv()
    for k in range(2):
        sol_ref[k * half : (k + 1) * half] = solbuf[k]

    for copy in swaps:
        copy.wait_send()
    for g in range(groups):
        mine = jnp.logical_and(is_last, plane == g)

        @pl.when(jnp.logical_and(useful, jnp.logical_not(mine)))
        def _(g=g):
            sep_copies(g).wait_send()

    @pl.when(jnp.logical_not(is_last))
    def _():
        y_copy.wait_send()
        u_copy.wait_send()

    to_earlier(lambda c, to: map_copy(c, to).wait_send())
    to_earlier(lambda c, to: turned_copy(c, to).wait_send())
    from_later(lambda c: map_onward(c, core).wait_send())

    @pl.when(is_last)
    def _():
        def sent(g, to):
            remote(rs_ref.at[mine_rows], rsbuf.at[plane], rs_s.at[g], rs_r.at[plane], to).wait_send()
            remote(idx_ref, idxbuf.at[plane], id_s.at[g], id_r.at[plane], to).wait_send()

        peers(sent)
        for copy in u_copies:
            copy.wait_send()
        for g in range(groups):
            part = sepbuf.at[g, core, pl.ds(skips[g], chips - skips[g])]
            remote(part, part, fwd_s.at[g], fwd_r.at[g], sibling).wait_send()
        for copy in z_copies:
            copy.wait_send()
        for copy in v_copies + so_copies:
            copy.wait_send()

    x_copy.wait_send()
    sx_copy.wait_send()


def solution(mesh):
    groups, fronts = mesh.shape["leaf"], mesh.shape["front"]
    chips = fronts // 2

    def shards(rhs_leaf, diag_inv, sub_block, coupling, update_rows, rhs_sep, sep_inv):
        width, columns = rhs_leaf.shape[1:]
        picks = coupling.shape[1]
        wide = rhs_sep.shape[0]
        deep = sep_inv.shape[0]
        rows = wide * groups
        half = columns // 2
        skips = tuple(g * wide // (2 * deep) for g in range(groups))
        vmem = pl.BlockSpec(memory_space=pltpu.VMEM)
        hbm = pl.BlockSpec(memory_space=pltpu.HBM)
        dma = pltpu.SemaphoreType.DMA
        out, sol = pl.pallas_call(
            functools.partial(kernel, groups, chips, skips),
            out_shape=(
                jax.ShapeDtypeStruct((columns, width), F32),
                jax.ShapeDtypeStruct((columns, wide), F32),
            ),
            in_specs=[hbm] * 7,
            out_specs=(vmem, vmem),
            scratch_shapes=[
                pltpu.VMEM((3, 2, width, width), BF16),
                pltpu.VMEM((2, 2, width, width), BF16),
                pltpu.VMEM((chips - 2, 2, 2, width, width), BF16),
                pltpu.VMEM((chips - 2, half, width), F32),
                pltpu.VMEM((half, width), F32),
                pltpu.VMEM((2, half, width), F32),
                pltpu.VMEM((3, half, width), F32),
                pltpu.VMEM((half, width), F32),
                pltpu.VMEM((half, picks), F32),
                pltpu.VMEM((half, picks), F32),
                pltpu.VMEM((groups, half, picks), F32),
                pltpu.VMEM((groups, half, wide), F32),
                pltpu.VMEM((groups, 1, picks), jnp.int32),
                pltpu.VMEM((groups, 2, chips, deep, wide), BF16),
                pltpu.VMEM((groups, rows, picks), BF16),
                pltpu.VMEM((2, half, chips * deep), F32),
                pltpu.VMEM((half, rows), F32),
                pltpu.VMEM((half, picks), F32),
                pltpu.VMEM((2, half, wide), F32),
                pltpu.VMEM((half, width), F32),
                pltpu.VMEM((half, width), F32),
                pltpu.VMEM((2, half, width), F32),
                pltpu.VMEM((2, half, width), F32),
                dma((6,)), dma((4,)), dma((4,)), dma, dma, dma, dma, dma((chips,)), dma,
                dma((groups,)), dma((groups,)), dma((groups,)), dma((groups,)),
                dma((groups,)), dma((groups,)), dma((groups,)), dma((groups,)),
                dma((groups,)), dma((groups,)),
                dma((chips,)), dma((chips,)), dma((chips,)), dma((chips,)), dma((chips,)), dma((chips,)),
                dma((chips,)), dma, dma((chips,)), dma, dma, dma, dma, dma,
            ],
            compiler_params=pltpu.CompilerParams(
                collective_id=0, has_side_effects=True, vmem_limit_bytes=64 * 1024 * 1024
            ),
        )(
            rhs_leaf[0].T, diag_inv[0, 0], sub_block[0, 0], coupling[0],
            update_rows, rhs_sep.T, sep_inv,
        )
        return out.T[None], sol.T

    return jax.shard_map(
        shards,
        mesh=mesh,
        in_specs=(
            P("leaf", "front", None),
            P("leaf", "front", None, None),
            P("leaf", "front", None, None),
            P("leaf", None, "front"),
            P("leaf", None),
            P("leaf", None),
            P("front", "leaf"),
        ),
        out_specs=(P("leaf", "front", None), P("leaf", None)),
        check_vma=False,
    )
```
